32 devices in a mesh: grp: 2 (over y), seq: 16 (over z, x, core).
Axes of the slice: x: 2, y: 2, z: 4, core: 2. Of those that a mesh axis runs over, the one named last changes fastest.
Arguments:
- queries: bfloat16 [4096, 64, 128], P(('grp', 'seq')), parts along dimension 0, may hold values from -6 to 6
- keys: bfloat16 [4096, 8, 128], P(('grp', 'seq')), parts along dimension 0, may hold values from -6 to 6
- values: bfloat16 [4096, 8, 128], P(('grp', 'seq')), parts along dimension 0, may hold values from -6 to 6
- house: bfloat16 [4096, 8, 128], P(('grp', 'seq')), parts along dimension 0, may hold values from -6 to 6
- beta: bfloat16 [4096, 8], P(('grp', 'seq')), parts along dimension 0, may hold values from 0.1 to 2
- forget_logit: bfloat16 [4096, 8], P(('grp', 'seq')), parts along dimension 0, may hold values from 0 to 9
- doc_lengths: int32 [16], P('grp'), parts along dimension 0, may hold values from 1 to 512, 2048 in all
Outputs:
- attended: bfloat16 [4096, 64, 128], P(('grp', 'seq')), parts along dimension 0
The draws below stay inside these ranges and needn't reach their ends.
There are 2 independent parts, one for each index of `grp`. The reference program is written for one: setup_inputs(seed, part) draws one part's arguments, and reference() takes and returns one part's arrays. A program takes and returns all parts, laid end to end along the dimension named above; each array names one. Nothing has to cross between parts.
Inputs may be any that keep to these rules, and one draw needn't show every extreme that they name: doc_lengths sum to 2048; the longest document has exactly 512 tokens.
All inputs are finite; a program needn't handle non-finite values.
Results may differ from the reference program's by a relative error of at most 0.0004.
Values may be sent and summed in bfloat16 or wider, within the bound.
A program may use at most 64 MiB of HBM per device.

```python
import math
import jax
import jax.numpy as jnp
import numpy as np
from jax import lax

TOK_DEV = 128
HQ = 64
KEY_VALUE_HEADS = 8
DH = 128
REACH = 4
PACKED_LENGTH = 2048
DOC_MOST = 512
NDOCS = 8
N_SEQ = 16


def draw_queries(key, part):
    root_seed = jnp.clip(jax.random.normal(jax.random.fold_in(key, 11), (PACKED_LENGTH, HQ, DH), jnp.float32), -6.0, 6.0)
    return root_seed.astype(jnp.bfloat16)


def draw_keys(key, part):
    root_seed = jnp.clip(jax.random.normal(jax.random.fold_in(key, 12), (PACKED_LENGTH, KEY_VALUE_HEADS, DH), jnp.float32), -6.0, 6.0)
    return root_seed.astype(jnp.bfloat16)


def draw_house(key, part):
    inner_key = jax.random.fold_in(key, 13)
    root_seed = jnp.clip(jax.random.normal(inner_key, (PACKED_LENGTH, KEY_VALUE_HEADS, DH), jnp.float32), -6.0, 6.0)
    return root_seed.astype(jnp.bfloat16)


def draw_beta(key, part):
    head_random_key, retain_random_key, spare_random_key = jax.random.split(jax.random.fold_in(key, 14), 3)
    share = 0.5
    keeping = jax.random.uniform(head_random_key, (KEY_VALUE_HEADS,), jnp.float32) < share
    strong = jax.random.uniform(retain_random_key, (PACKED_LENGTH, KEY_VALUE_HEADS), jnp.float32, 1.8, 2.0)
    loose = jax.random.uniform(spare_random_key, (PACKED_LENGTH, KEY_VALUE_HEADS), jnp.float32, 0.1, 1.9)
    return jnp.where(keeping[None, :], strong, loose).astype(jnp.bfloat16)


def draw_forget_logit(key, part):
    head_random_key, retain_random_key, spare_random_key, spike_random_key, height_random_key = jax.random.split(jax.random.fold_in(key, 15), 5)
    share = 0.5
    keeping = jax.random.uniform(head_random_key, (KEY_VALUE_HEADS,), jnp.float32) < share
    slow = jax.random.uniform(retain_random_key, (PACKED_LENGTH, KEY_VALUE_HEADS), jnp.float32, 7.0, 9.0)
    fast = jax.random.uniform(spare_random_key, (PACKED_LENGTH, KEY_VALUE_HEADS), jnp.float32, 2.8, 4.0)
    root_seed = jnp.where(keeping[None, :], slow, fast)
    spike_events = jax.random.uniform(spike_random_key, (PACKED_LENGTH,), jnp.float32) < 0.003
    spike_height = jax.random.uniform(height_random_key, (PACKED_LENGTH, KEY_VALUE_HEADS), jnp.float32, 0.0, 1.4)
    return jnp.where(spike_events[:, None], spike_height, root_seed).astype(jnp.bfloat16)


def block_levels(key, extent, shards, least, largest):
    level, own = 1.0, jax.random.fold_in(key, 6)
    for position, parts in shards:
        heights = jnp.exp(jax.random.uniform(jax.random.fold_in(own, position), (parts,), jnp.float32, least / len(shards), largest / len(shards)))
        level = level * jnp.repeat(heights, extent[position] // parts).reshape([-1 if axis == position else 1 for axis in range(len(extent))])
    return level


def length_profile(amount, total, bound, lean):
    loads = [(1 << 20) // math.isqrt(rank ** lean) + 1 for rank in range(2, amount + 1)]
    rest, counts = total - bound - (amount - 1), [1] * (amount - 1)
    while rest > 0:
        movable = [i for i in range(amount - 1) if counts[i] < bound]
        whole, remaining = sum([loads[i] for i in movable]), rest
        for i in movable:
            more = min(bound - counts[i], max(1, remaining * loads[i] // whole), rest)
            counts[i] = counts[i] + more
            rest = rest - more
    return np.array([bound] + counts)


def ragged(key, count, total, most, slope):
    if count == 2:
        one = jax.random.randint(key, (), max(1, total - most), min(most, total - 1) + 1)
        return jnp.stack([one, total - one])
    tallies = jnp.asarray(length_profile(count, total, most, slope), jnp.int32)
    pairs = (count - 1) // 2
    donor, receiver = tallies[1:1 + 2 * pairs:2], tallies[2:2 + 2 * pairs:2]
    room = jnp.minimum(donor - 1, most - receiver)
    shifted = jax.random.randint(jax.random.fold_in(key, 1), (pairs,), 0, 1 << 20) % (room + 1)
    tallies = tallies.at[1:1 + 2 * pairs:2].set(donor - shifted).at[2:2 + 2 * pairs:2].set(receiver + shifted)
    return tallies[jax.random.permutation(jax.random.fold_in(key, 2), count)]


def scatter_about(rng, shape, spread, bound, pieces=(), held_as=jnp.bfloat16):
    factor_of = block_levels(rng, shape, pieces, -0.22, 0.18) if pieces else 1.0
    drawn = jax.random.normal(rng, shape, jnp.float32) * spread * factor_of
    return jnp.minimum(jnp.maximum(drawn, -bound), bound).astype(held_as)


def setup_inputs(seed: int = 0, part: int = 0) -> dict:
    splits = jax.random.split(jax.random.key(seed), 8)
    own_keys = jax.random.split(jax.random.fold_in(splits[7], part), 8)
    return {
        "queries": draw_queries(jax.random.fold_in(jax.random.fold_in(splits[7], part), 71), part),
        "keys": draw_keys(jax.random.fold_in(jax.random.fold_in(splits[7], part), 71), part),
        "values": scatter_about(own_keys[2], (PACKED_LENGTH, KEY_VALUE_HEADS, DH), 1.0, 6.0, ((0, 16),)),
        "house": draw_house(jax.random.fold_in(jax.random.fold_in(splits[7], part), 71), part),
        "beta": draw_beta(jax.random.fold_in(jax.random.fold_in(splits[7], part), 71), part),
        "forget_logit": draw_forget_logit(jax.random.fold_in(jax.random.fold_in(splits[7], part), 71), part),
        "doc_lengths": ragged(own_keys[6], NDOCS, PACKED_LENGTH, DOC_MOST, 1).astype(jnp.int32),
    }


HIGH = lax.Precision.HIGHEST
NEG = -1e+30

def join_gate(earlier, later):
    return (jnp.where(later[1] > 0.5, later[0], earlier[0] + later[0]), jnp.maximum(earlier[1], later[1]))

def shift_blocks(array, fill):
    pad_block = jnp.full((1,) + array.shape[1:], fill, array.dtype)
    return jnp.concatenate([pad_block, array[:-1]], axis=0)

def apply_product(carried, unit_vec, factor):
    projected = jnp.einsum('bjhd,bahd->bhja', carried, unit_vec, precision=HIGH)
    mixed = jnp.einsum('bhja,bhac->bhjc', projected, factor, precision=HIGH)
    return carried - jnp.einsum('bhjc,bchd->bjhd', mixed, unit_vec, precision=HIGH)

def merge_block(state, scores, valid, vals):
    peak_old, total, accum = state
    masked = jnp.where(valid, scores, NEG)
    peak = jnp.maximum(peak_old, lax.optimization_barrier(jnp.max(masked, axis=-1)))
    rescale = jnp.exp(peak_old - peak)
    weights = jnp.where(valid, jnp.exp(masked - peak[..., None]), 0.0)
    total = rescale * total + lax.optimization_barrier(jnp.sum(weights, axis=-1))
    accum = rescale[..., None] * accum + jnp.einsum('bhgij,bjhd->bhgid', weights, vals, precision=HIGH)
    return (peak, total, accum)

def gate_bias(gate_rows, gate_cols):
    return jnp.transpose(gate_rows, (0, 2, 1))[:, :, None, :, None] - jnp.transpose(gate_cols, (0, 2, 1))[:, :, None, None, :]

def reference(queries, keys, values, house, beta, forget_logit, doc_lengths):
    blocks = N_SEQ
    count = TOK_DEV
    group = HQ // KEY_VALUE_HEADS
    inv_scale = 1.0 / DH ** 0.5
    q_full = queries.astype(jnp.float32).reshape(blocks, count, KEY_VALUE_HEADS, group, DH)
    k_full = keys.astype(jnp.float32).reshape(blocks, count, KEY_VALUE_HEADS, DH)
    v_full = values.astype(jnp.float32).reshape(blocks, count, KEY_VALUE_HEADS, DH)
    unit_vec = house.astype(jnp.float32)
    unit_vec = unit_vec * lax.rsqrt(lax.optimization_barrier(jnp.sum(unit_vec * unit_vec, axis=-1, keepdims=True)) + 1e-06)
    unit_vec = unit_vec.reshape(blocks, count, KEY_VALUE_HEADS, DH)
    beta_full = beta.astype(jnp.float32).reshape(blocks, count, KEY_VALUE_HEADS)
    log_gate = jax.nn.log_sigmoid(forget_logit.astype(jnp.float32))
    positions = jnp.arange(PACKED_LENGTH, dtype=jnp.int32)
    starts = (jnp.cumsum(doc_lengths) - doc_lengths).astype(jnp.int32)
    doc_ids = lax.optimization_barrier(jnp.sum((starts[None, :] <= positions[:, None]).astype(jnp.int32), axis=1)).astype(jnp.int32) - 1
    start_flag = jnp.any(starts[None, :] == positions[:, None], axis=1).astype(log_gate.dtype)
    flags = jnp.broadcast_to(start_flag[:, None], log_gate.shape)
    gate_sum, unused_flag = lax.associative_scan(join_gate, (log_gate, flags), axis=0)
    gate_sum = gate_sum.reshape(blocks, count, KEY_VALUE_HEADS)
    doc_block = doc_ids.reshape(blocks, count)
    index_row = lax.broadcasted_iota(jnp.int32, (count, count), 0)
    index_col = lax.broadcasted_iota(jnp.int32, (count, count), 1)
    identity = (index_row == index_col).astype(q_full.dtype)
    gram_matrix = jnp.einsum('bahd,bchd->bhac', unit_vec, unit_vec, precision=HIGH)
    system = jnp.where(index_col > index_row, gram_matrix, 0.0) + identity * jnp.transpose(1.0 / beta_full, (0, 2, 1))[:, :, :, None]
    factor = jax.scipy.linalg.solve_triangular(system, jnp.broadcast_to(identity, system.shape), lower=False)
    lower_incl = (index_col <= index_row).astype(q_full.dtype)
    strict_later = (index_col > index_row).astype(q_full.dtype)
    proj_q = jnp.einsum('bihgd,bchd->bhgic', q_full, unit_vec, precision=HIGH) * lower_incl
    mixed_q = jnp.einsum('bhgic,bhac->bhgia', proj_q, factor, precision=HIGH)
    q_hat = q_full - jnp.einsum('bhgia,bahd->bihgd', mixed_q, unit_vec, precision=HIGH)
    proj_k = jnp.einsum('bjhd,bahd->bhja', k_full, unit_vec, precision=HIGH) * strict_later
    mixed_k = jnp.einsum('bhja,bhac->bhjc', proj_k, factor, precision=HIGH)
    suffix = k_full - jnp.einsum('bhjc,bchd->bjhd', mixed_k, unit_vec, precision=HIGH)
    intra = jnp.einsum('bihgd,bjhd->bhgij', q_full, k_full, precision=HIGH) - jnp.einsum('bhgia,bhja->bhgij', mixed_q, proj_k, precision=HIGH)
    intra = intra * inv_scale + gate_bias(gate_sum, gate_sum)
    same_doc = (doc_block[:, :, None] == doc_block[:, None, :]) & (index_col <= index_row)[None]
    state = (jnp.full((blocks, KEY_VALUE_HEADS, group, count), NEG, q_full.dtype), jnp.zeros((blocks, KEY_VALUE_HEADS, group, count), q_full.dtype), jnp.zeros((blocks, KEY_VALUE_HEADS, group, count, DH), q_full.dtype))
    state = merge_block(state, intra, same_doc[:, None, None], v_full)
    cur_keys = shift_blocks(suffix, 0.0)
    cur_vals = shift_blocks(v_full, 0.0)
    cur_gate = shift_blocks(gate_sum, 0.0)
    cur_doc = shift_blocks(doc_block, -1)
    for hop_index in range(REACH):
        scores = jnp.einsum('bihgd,bjhd->bhgij', q_hat, cur_keys, precision=HIGH) * inv_scale + gate_bias(gate_sum, cur_gate)
        valid = (doc_block[:, :, None] == cur_doc[:, None, :])[:, None, None]
        state = merge_block(state, scores, valid, cur_vals)
        cur_keys = shift_blocks(apply_product(cur_keys, unit_vec, factor), 0.0)
        cur_vals = shift_blocks(cur_vals, 0.0)
        cur_gate = shift_blocks(cur_gate, 0.0)
        cur_doc = shift_blocks(cur_doc, -1)
    peak, total, accum = state
    result = accum / total[..., None]
    result = jnp.transpose(result, (0, 3, 1, 2, 4)).reshape(PACKED_LENGTH, HQ, DH)
    return result.astype(jnp.bfloat16)
```

```python
import functools
import jax
import jax.numpy as jnp
from jax import lax
from jax.experimental import pallas as pl
from jax.experimental.pallas import tpu as pltpu
from jax.sharding import PartitionSpec as P

REACH = 4
NEG = -1e30
LOG2E = 1.4426950408889634
BF = jnp.bfloat16
F32 = jnp.float32


def halves(x):
    hi = x.astype(BF)
    return hi, (x - hi.astype(F32)).astype(BF)


def dot(a, b):
    return jnp.dot(a, b, preferred_element_type=F32)


def dot_nt(a, b):
    return lax.dot_general(a, b, (((1,), (1,)), ((), ())), preferred_element_type=F32)


def left3(x):
    hi, lo = halves(x)
    return jnp.concatenate([hi, lo, hi], axis=1)


def right3(x):
    hi, lo = halves(x)
    return jnp.concatenate([hi, hi, lo], axis=0)


def left2(x):
    hi, lo = halves(x)
    return jnp.concatenate([hi, lo], axis=1)


def inverses(systems, betas):
    length = systems[0].shape[0]
    row = lax.broadcasted_iota(jnp.int32, (length, length), 0)
    col = lax.broadcasted_iota(jnp.int32, (length, length), 1)
    heads = range(len(systems))
    invs = [jnp.where(row == col, betas[h], 0.0) for h in heads]
    first = (row + 1 == col) & (row % 2 == 0)
    rows = [jnp.sum(inv, axis=0, keepdims=True) for inv in invs]
    invs = [
        invs[h] - jnp.where(first, betas[h] * systems[h] * rows[h], 0.0) for h in heads
    ]
    width = 2
    while width < length:
        corner = (
            (row // (2 * width) == col // (2 * width))
            & (row // width % 2 == 0)
            & (col // width % 2 == 1)
        )
        links = [right3(jnp.where(corner, systems[h], 0.0)) for h in heads]
        parts = [dot(left3(invs[h]), links[h]) for h in heads]
        invs = [invs[h] - dot(left3(parts[h]), right3(invs[h])) for h in heads]
        width *= 2
    return invs


def prep_kernel(k_ref, v_ref, u_ref, beta_ref, gate_ref, kx_ref, vt_ref, uk_ref, w_ref, p_ref, suf_ref, pre_ref, tot_ref):
    count, heads, dim = k_ref.shape
    row = lax.broadcasted_iota(jnp.int32, (count, count), 0)
    col = lax.broadcasted_iota(jnp.int32, (count, count), 1)
    kf = pltpu.einshape("mhd->hmd", k_ref[...].astype(F32))
    uf = pltpu.einshape("mhd->hmd", u_ref[...].astype(F32))
    vf = pltpu.einshape("mhd->hmd", v_ref[...].astype(F32))
    vt_ref[...] = vf.astype(BF)
    logit = gate_ref[...].astype(F32)
    gate = (jnp.minimum(logit, 0.0) - jnp.log1p(jnp.exp(-jnp.abs(logit)))) * LOG2E
    g1, g2 = halves(gate)
    g3 = (gate - g1.astype(F32) - g2.astype(F32)).astype(BF)
    pieces = jnp.concatenate([g1, g2, g3], axis=1)
    later = (row > col).astype(F32).astype(BF)
    upto = (row <= col).astype(F32).astype(BF)
    every = jnp.ones((count, count), BF)
    suf_ref[...] = dot(pieces, jnp.concatenate([later] * 3, axis=0))
    pre_ref[...] = dot(pieces, jnp.concatenate([upto] * 3, axis=0))
    tot_ref[...] = dot(pieces, jnp.concatenate([every] * 3, axis=0))
    beta = beta_ref[...].astype(F32)
    us = [uf[h].astype(BF) for h in range(heads)]
    ks = [kf[h].astype(BF) for h in range(heads)]
    betas = [
        beta[:, h : h + 1] / (jnp.sum(uf[h] * uf[h], axis=1, keepdims=True) + 1e-06)
        for h in range(heads)
    ]
    systems = [dot_nt(us[h], us[h]) for h in range(heads)]
    invs = inverses(systems, betas)
    for h in range(heads):
        u, k = us[h], ks[h]
        uu = jnp.concatenate([u, u], axis=0)
        fu = dot(left2(invs[h]), uu)
        proj = jnp.where(col > row, dot_nt(k, u), 0.0)
        suffix = kf[h] - dot(left3(proj), right3(fu))
        hi, lo = halves(suffix)
        kx_ref[h] = jnp.concatenate([hi, lo], axis=1)
        ut = uf[h].T.astype(BF)
        fhi, flo = halves(fu)
        move = jnp.where(row == col, 1.0, 0.0) - dot(
            jnp.concatenate([ut, ut], axis=1), jnp.concatenate([fhi, flo], axis=0)
        )
        p_ref[h] = right3(move)
        ft = invs[h].T
        projt = jnp.where(row > col, dot_nt(u, k), 0.0)
        w1 = dot(left2(ft), uu)
        w2 = dot(left3(ft), right3(projt))
        w_ref[h] = right3(jnp.concatenate([w1, w2], axis=1))
        uk_ref[h] = jnp.concatenate([u, k], axis=0)


def advance_kernel(kx_ref, p_ref, bias_ref, tot_ref, out_ref, bias_out):
    dim = p_ref.shape[2]
    bias_out[...] = bias_ref[...] + tot_ref[...]
    for h in range(kx_ref.shape[0]):
        x = kx_ref[h]
        moved = dot(jnp.concatenate([x, x[:, :dim]], axis=1), p_ref[h])
        hi, lo = halves(moved)
        out_ref[h] = jnp.concatenate([hi, lo], axis=1)


def attend_kernel(docs_ref, q_ref, uk_ref, w_ref, *refs):
    kxs, vs, biases = refs[:REACH], refs[REACH : 2 * REACH + 1], refs[2 * REACH + 1 : 3 * REACH + 2]
    out_ref, own_mask, row_mask, col_mask = refs[3 * REACH + 2 :]
    h = pl.program_id(0)
    count, group, dim = q_ref.shape
    rows = count * group
    token = lax.broadcasted_iota(jnp.int32, (rows, count), 0) // group
    key = lax.broadcasted_iota(jnp.int32, (rows, count), 1)
    base = lax.axis_index("seq") * count

    @pl.when(h == 0)
    def _():
        own_mask[...] = jnp.where(key <= token, 0.0, NEG)

        def one(n, carry):
            start, s_prev, e_prev = carry
            end = start + docs_ref[n]
            holds = start < base
            s_prev = jnp.where(holds, start, s_prev)
            e_prev = jnp.where(holds, end, e_prev)

            @pl.when((start > base) & (start < base + count))
            def _():
                local = start - base
                own_mask[...] = jnp.where((token >= local) & (key < local), NEG, own_mask[...])

            return end, s_prev, e_prev

        _, s_prev, e_prev = lax.fori_loop(0, docs_ref.shape[0], one, (0, 0, 0))
        row_mask[...] = jnp.where(base + token < e_prev, 0.0, NEG)
        spot = lax.broadcasted_iota(jnp.int32, (8, REACH * count), 1)
        place = base - count * (1 + spot // count) + spot % count
        col_mask[...] = jnp.where(place >= s_prev, 0.0, NEG)

    scale = LOG2E / dim**0.5
    qf = q_ref[...].astype(F32).reshape(rows, dim)
    both = dot_nt(qf.astype(BF), uk_ref[0])
    proj = jnp.where(key <= token, both[:, :count], 0.0)
    fix = dot(left3(proj), w_ref[0])
    q_hat = (qf - fix[:, :dim]) * scale
    intra = (both[:, count:] - fix[:, dim:]) * scale + own_mask[...] - biases[0][pl.ds(h, 1), :]
    ql = left3(q_hat)
    parts = [intra]
    for n in range(REACH):
        kx = kxs[n][0]
        kr = jnp.concatenate([kx[:, :dim], kx[:, :dim], kx[:, dim:]], axis=1)
        bias = biases[n + 1][pl.ds(h, 1), :] + col_mask[0:1, n * count : (n + 1) * count]
        parts.append(dot_nt(ql, kr) + bias + row_mask[...])
    peak = functools.reduce(jnp.maximum, parts)
    peak = jnp.max(peak, axis=1, keepdims=True)
    his, los = [], []
    for part in parts:
        hi, lo = halves(jnp.exp2(part - peak))
        his.append(hi)
        los.append(lo)
    weights = jnp.concatenate(his + los, axis=1)
    vals = jnp.concatenate([v[0] for v in vs], axis=0)
    vals = jnp.concatenate([vals, jnp.ones_like(vals)], axis=1)
    acc = dot(weights, jnp.concatenate([vals, vals], axis=0))
    out = acc[:, :dim] / acc[:, dim:]
    out_ref[...] = out.reshape(count, group, dim).astype(BF)


def passed_along(block, axis):
    size = lax.axis_size(axis)
    return lax.ppermute(block, axis, [(i, i + 1) for i in range(size - 1)])


def shards(queries, keys, values, house, beta, forget_logit, doc_lengths):
    count, heads, dim = keys.shape
    group = queries.shape[1] // heads
    sds = jax.ShapeDtypeStruct
    params = pltpu.CompilerParams(vmem_limit_bytes=48 << 20)
    kx, vt, uk, w, p, suf, pre, tot = pl.pallas_call(
        prep_kernel,
        out_shape=[
            sds((heads, count, 2 * dim), BF),
            sds((heads, count, dim), BF),
            sds((heads, 2 * count, dim), BF),
            sds((heads, 3 * count, dim + count), BF),
            sds((heads, 3 * dim, dim), BF),
            sds((heads, count), F32),
            sds((heads, count), F32),
            sds((heads, count), F32),
        ],
        compiler_params=params,
    )(keys, values, house, beta, forget_logit.T)
    kxs, vs, biases = [], [vt], [pre]
    bias, vals = suf, vt
    for hop in range(REACH):
        kx = passed_along(kx, "seq")
        bias = passed_along(bias, "seq")
        vals = passed_along(vals, "seq")
        kxs.append(kx)
        vs.append(vals)
        biases.append(bias)
        if hop < REACH - 1:
            kx, bias = pl.pallas_call(
                advance_kernel,
                out_shape=[sds(kx.shape, BF), sds(bias.shape, F32)],
                compiler_params=params,
            )(kx, p, bias, tot)
    rows = count * group

    def head(*shape):
        return pl.BlockSpec((1,) + shape, lambda h: (h,) + (0,) * len(shape))

    whole = pl.BlockSpec((heads, count), lambda h: (0, 0))
    q_spec = pl.BlockSpec((count, group, dim), lambda h: (0, h, 0))
    return pl.pallas_call(
        attend_kernel,
        grid=(heads,),
        in_specs=[
            pl.BlockSpec(memory_space=pltpu.SMEM),
            q_spec,
            head(2 * count, dim),
            head(3 * count, dim + count),
        ]
        + [head(count, 2 * dim)] * REACH
        + [head(count, dim)] * (REACH + 1)
        + [whole] * (REACH + 1),
        out_specs=q_spec,
        out_shape=sds((count, heads * group, dim), BF),
        scratch_shapes=[
            pltpu.VMEM((rows, count), F32),
            pltpu.VMEM((rows, count), F32),
            pltpu.VMEM((8, REACH * count), F32),
        ],
        compiler_params=params,
    )(doc_lengths, queries, uk, w, *kxs, *vs, *biases)


def solution(mesh):
    placed = (
        P(("grp", "seq"), None, None),
        P(("grp", "seq"), None, None),
        P(("grp", "seq"), None, None),
        P(("grp", "seq"), None, None),
        P(("grp", "seq"), None),
        P(("grp", "seq"), None),
        P("grp"),
    )
    return jax.shard_map(
        shards, mesh=mesh, in_specs=placed, out_specs=P(("grp", "seq"), None, None), check_vma=False
    )
```

```python
import functools
import jax
import jax.numpy as jnp
from jax import lax
from jax.experimental import pallas as pl
from jax.experimental.pallas import tpu as pltpu
from jax.sharding import PartitionSpec as P

REACH = 4
NEG = -1e30
LOG2E = 1.4426950408889634
BF = jnp.bfloat16
F32 = jnp.float32


def halves(x):
    hi = x.astype(BF)
    return hi, (x - hi.astype(F32)).astype(BF)


def dot(a, b):
    return jnp.dot(a, b, preferred_element_type=F32)


def dot_nt(a, b):
    return lax.dot_general(a, b, (((1,), (1,)), ((), ())), preferred_element_type=F32)


def left3(x):
    hi, lo = halves(x)
    return jnp.concatenate([hi, lo, hi], axis=1)


def right3(x):
    hi, lo = halves(x)
    return jnp.concatenate([hi, hi, lo], axis=0)


def left2(x):
    hi, lo = halves(x)
    return jnp.concatenate([hi, lo], axis=1)


def inverses(systems, betas):
    length = systems[0].shape[0]
    row = lax.broadcasted_iota(jnp.int32, (length, length), 0)
    col = lax.broadcasted_iota(jnp.int32, (length, length), 1)
    heads = range(len(systems))
    invs = [jnp.where(row == col, betas[h], 0.0) for h in heads]
    first = (row + 1 == col) & (row % 2 == 0)
    rows = [jnp.sum(inv, axis=0, keepdims=True) for inv in invs]
    invs = [
        invs[h] - jnp.where(first, betas[h] * systems[h] * rows[h], 0.0) for h in heads
    ]
    width = 2
    while width < length:
        corner = (
            (row // (2 * width) == col // (2 * width))
            & (row // width % 2 == 0)
            & (col // width % 2 == 1)
        )
        links = [right3(jnp.where(corner, systems[h], 0.0)) for h in heads]
        parts = [dot(left3(invs[h]), links[h]) for h in heads]
        invs = [invs[h] - dot(left3(parts[h]), right3(invs[h])) for h in heads]
        width *= 2
    return invs


CHUNKS = 2


def fused_kernel(
    docs_ref, gate_ref, beta_ref, k_ref, v_ref, u_ref, q_hbm, out_hbm,
    q_buf, o_buf, k_send, k_got, vals, b_send, b_got, tots, uks, ws, moves, qls, intras, accs, peaks,
    own_mask, row_mask, col_mask,
    q_sem, o_sem, ks_sem, kr_sem, vs_sem, vr_sem, bs_sem, br_sem,
):
    count, heads, dim = k_ref.shape
    group = q_buf.shape[2]
    rows = count * group
    span = heads // CHUNKS
    me, last = lax.axis_index("seq"), lax.axis_size("seq") - 1
    right, left = jnp.minimum(me + 1, last), jnp.maximum(me - 1, 0)
    has_right, has_left = me < last, me > 0

    def remote(src, dst, send, recv):
        return pltpu.make_async_remote_copy(
            src_ref=src, dst_ref=dst, send_sem=send, recv_sem=recv,
            device_id={"seq": right}, device_id_type=pl.DeviceIdType.MESH,
        )

    def k_copy(hop, c):
        part = pl.ds(c * span, span)
        return remote(
            k_send.at[hop - 1, part], k_got.at[hop - 1, part], ks_sem.at[hop - 1, c], kr_sem.at[hop - 1, c]
        )

    def v_copy(hop):
        return remote(vals.at[hop - 1], vals.at[hop], vs_sem.at[hop - 1], vr_sem.at[hop - 1])

    def b_copy(hop):
        return remote(b_send.at[hop - 1], b_got.at[hop - 1], bs_sem.at[hop - 1], br_sem.at[hop - 1])

    def start(copy):
        @pl.when(has_right)
        def _():
            copy.start()

    def got(copy):
        @pl.when(has_left)
        def _():
            copy.wait_recv()

    def q_copy(h):
        return pltpu.make_async_copy(q_hbm.at[:, pl.ds(h * group, group), :], q_buf.at[h], q_sem.at[h])

    def o_copy(h):
        return pltpu.make_async_copy(o_buf.at[h], out_hbm.at[:, pl.ds(h * group, group), :], o_sem.at[h])

    barrier = pltpu.get_barrier_semaphore()

    @pl.when(has_left)
    def _():
        pl.semaphore_signal(barrier, inc=1, device_id={"seq": left}, device_id_type=pl.DeviceIdType.MESH)

    @pl.when(has_right)
    def _():
        pl.semaphore_signal(barrier, inc=1, device_id={"seq": right}, device_id_type=pl.DeviceIdType.MESH)

    for h in range(heads):
        q_copy(h).start()

    @pl.when(jnp.logical_not(has_left))
    def _():
        k_got[...] = jnp.zeros_like(k_got)
        b_got[...] = jnp.zeros_like(b_got)
        vals[pl.ds(1, REACH)] = jnp.zeros((REACH,) + vals.shape[1:], BF)

    vals[0] = pltpu.einshape("mhd->hmd", v_ref[...].astype(F32)).astype(BF)
    row = lax.broadcasted_iota(jnp.int32, (count, count), 0)
    col = lax.broadcasted_iota(jnp.int32, (count, count), 1)
    logit = gate_ref[...].astype(F32)
    gate = (jnp.minimum(logit, 0.0) - jnp.log1p(jnp.exp(-jnp.abs(logit)))) * LOG2E
    g1, g2 = halves(gate)
    g3 = (gate - g1.astype(F32) - g2.astype(F32)).astype(BF)
    pieces = jnp.concatenate([g1, g2, g3], axis=1)

    def summed(mask):
        return dot(pieces, jnp.concatenate([mask.astype(F32).astype(BF)] * 3, axis=0))

    b_send[0] = summed(row > col)
    tots[0] = summed(row <= col)
    tots[1] = summed(row >= 0)

    @pl.when(has_left & has_right)
    def _():
        pl.semaphore_wait(barrier, 2)

    @pl.when(jnp.logical_not(has_left & has_right))
    def _():
        pl.semaphore_wait(barrier, 1)

    start(v_copy(1))
    start(b_copy(1))

    kf = pltpu.einshape("mhd->hmd", k_ref[...].astype(F32))
    uf = pltpu.einshape("mhd->hmd", u_ref[...].astype(F32))
    beta = beta_ref[...].astype(F32)
    us = [uf[h].astype(BF) for h in range(heads)]
    ks = [kf[h].astype(BF) for h in range(heads)]
    betas = [
        beta[:, h : h + 1] / (jnp.sum(uf[h] * uf[h], axis=1, keepdims=True) + 1e-06)
        for h in range(heads)
    ]
    invs = inverses([dot_nt(us[h], us[h]) for h in range(heads)], betas)
    fus = []
    for c in range(CHUNKS):
        for h in range(c * span, (c + 1) * span):
            fu = dot(left2(invs[h]), jnp.concatenate([us[h], us[h]], axis=0))
            fus.append(fu)
            proj = jnp.where(col > row, dot_nt(ks[h], us[h]), 0.0)
            hi, lo = halves(kf[h] - dot(left3(proj), right3(fu)))
            k_send[0, h] = jnp.concatenate([hi, lo], axis=1)
        start(k_copy(1, c))
    got(v_copy(1))
    start(v_copy(2))
    for h in range(heads):
        ut = uf[h].T.astype(BF)
        fhi, flo = halves(fus[h])
        move = jnp.where(row == col, 1.0, 0.0) - dot(
            jnp.concatenate([ut, ut], axis=1), jnp.concatenate([fhi, flo], axis=0)
        )
        moves[h] = right3(move)
        ft = invs[h].T
        projt = jnp.where(row > col, dot_nt(us[h], ks[h]), 0.0)
        w1 = dot(left2(ft), jnp.concatenate([us[h], us[h]], axis=0))
        w2 = dot(left3(ft), right3(projt))
        ws[h] = right3(jnp.concatenate([w1, w2], axis=1))
        uks[h] = jnp.concatenate([us[h], ks[h]], axis=0)

    token = lax.broadcasted_iota(jnp.int32, (rows, count), 0) // group
    key = lax.broadcasted_iota(jnp.int32, (rows, count), 1)
    scale = LOG2E / dim**0.5

    def query_side(h, carry):
        q_copy(h).wait()
        qf = q_buf[h].astype(F32).reshape(rows, dim)
        both = dot_nt(qf.astype(BF), uks[h])
        proj = jnp.where(key <= token, both[:, :count], 0.0)
        fix = dot(left3(proj), ws[h])
        qls[h] = left2((qf - fix[:, :dim]) * scale)
        intras[h] = (both[:, count:] - fix[:, dim:]) * scale
        return carry

    def pass_on(hop, c):
        got(k_copy(hop, c))
        if hop == REACH:
            return
        for h in range(c * span, (c + 1) * span):
            x = k_got[hop - 1, h]
            hi, lo = halves(dot(jnp.concatenate([x, x[:, :dim]], axis=1), moves[h]))
            k_send[hop, h] = jnp.concatenate([hi, lo], axis=1)
        start(k_copy(hop + 1, c))

    def pass_bias(hop):
        got(b_copy(hop))
        if hop < REACH:
            b_send[hop] = b_got[hop - 1] + tots[1]
            start(b_copy(hop + 1))

    def masks():
        base = me * count

        def one(n, carry):
            begin, s_prev, e_prev, bad = carry
            end = begin + docs_ref[n]
            holds = begin < base
            s_prev = jnp.where(holds, begin, s_prev)
            e_prev = jnp.where(holds, end, e_prev)
            local = begin - base
            bad = jnp.where((token >= local) & (key < local), NEG, bad)
            return end, s_prev, e_prev, bad

        zero = jnp.int32(0)
        _, s_prev, e_prev, bad = lax.fori_loop(
            0, docs_ref.shape[0], one, (zero, zero, zero, jnp.where(key <= token, 0.0, NEG))
        )
        own_mask[...] = bad
        row_mask[...] = jnp.where(base + token < e_prev, 0.0, NEG)
        spot = lax.broadcasted_iota(jnp.int32, (8, REACH * count), 1)
        place = base - count * (1 + spot // count) + spot % count
        col_mask[...] = jnp.where(place >= s_prev, 0.0, NEG)

    def hop_scores(h, hop):
        ql = qls[h]
        ql = jnp.concatenate([ql, ql[:, :dim]], axis=1)
        pair = jnp.concatenate([k_got[hop - 1, h], k_got[hop, h]], axis=0)
        pair = jnp.concatenate([pair[:, :dim], pair], axis=1)
        both = dot_nt(ql, pair)
        parts = []
        for n in range(2):
            at = (hop - 1 + n) * count
            bias = b_got[hop - 1 + n, pl.ds(h, 1), :] + col_mask[0:1, at : at + count]
            parts.append(both[:, n * count : (n + 1) * count] + bias + row_mask[...])
        return parts

    def weigh(parts, peak, blocks):
        his, los = [], []
        for part in parts:
            hi, lo = halves(jnp.exp2(part - peak))
            his.append(hi)
            los.append(lo)
        stack = jnp.concatenate(blocks, axis=0)
        stack = jnp.concatenate([stack, jnp.ones_like(stack)], axis=1)
        return dot(jnp.concatenate(his + los, axis=1), jnp.concatenate([stack, stack], axis=0))

    def near(h, carry):
        parts = [intras[h] + own_mask[...] - tots[0, pl.ds(h, 1), :]] + hop_scores(h, 1)
        peak = jnp.max(functools.reduce(jnp.maximum, parts), axis=1, keepdims=True)
        accs[h] = weigh(parts, peak, [vals[n, h] for n in range(3)])
        peaks[h] = jnp.broadcast_to(peak, (rows, count))
        return carry

    def far(h, carry):
        parts = hop_scores(h, 3)
        old = peaks[h]
        peak = jnp.max(functools.reduce(jnp.maximum, parts + [old]), axis=1, keepdims=True)
        acc = weigh(parts, peak, [vals[n, h] for n in range(3, 5)])
        fade = jnp.exp2(old - peak)
        top = acc[:, :dim] + fade * accs[h, :, :dim]
        low = acc[:, dim:] + fade * accs[h, :, dim:]
        o_buf[h] = (top / low).reshape(count, group, dim).astype(BF)
        o_copy(h).start()
        return carry

    lax.fori_loop(0, 2, query_side, 0)
    pass_on(1, 0)
    pass_bias(1)
    got(v_copy(2))
    start(v_copy(3))
    lax.fori_loop(2, 3, query_side, 0)
    pass_on(1, 1)
    lax.fori_loop(3, 5, query_side, 0)
    pass_on(2, 0)
    pass_bias(2)
    lax.fori_loop(5, 7, query_side, 0)
    pass_on(2, 1)
    got(v_copy(3))
    start(v_copy(4))
    masks()
    lax.fori_loop(7, heads, query_side, 0)
    lax.fori_loop(0, 1, near, 0)
    pass_on(3, 0)
    pass_bias(3)
    lax.fori_loop(1, 3, near, 0)
    pass_on(3, 1)
    lax.fori_loop(3, heads, near, 0)
    pass_bias(4)
    got(v_copy(4))
    for c in range(CHUNKS):
        pass_on(4, c)
        lax.fori_loop(c * span, (c + 1) * span, far, 0)

    @pl.when(has_right)
    def _():
        for hop in range(1, REACH + 1):
            v_copy(hop).wait_send()
            b_copy(hop).wait_send()
            for c in range(CHUNKS):
                k_copy(hop, c).wait_send()

    for h in range(heads):
        o_copy(h).wait()


def shards(queries, keys, values, house, beta, forget_logit, doc_lengths):
    count, heads, dim = keys.shape
    group = queries.shape[1] // heads
    rows = count * group
    vmem = pl.BlockSpec(memory_space=pltpu.VMEM)
    hbm = pl.BlockSpec(memory_space=pl.ANY)
    dma = pltpu.SemaphoreType.DMA
    return pl.pallas_call(
        fused_kernel,
        in_specs=[pl.BlockSpec(memory_space=pltpu.SMEM)] + [vmem] * 5 + [hbm],
        out_specs=hbm,
        out_shape=jax.ShapeDtypeStruct(queries.shape, BF),
        scratch_shapes=[
            pltpu.VMEM((heads, count, group, dim), BF),
            pltpu.VMEM((heads, count, group, dim), BF),
            pltpu.VMEM((REACH, heads, count, 2 * dim), BF),
            pltpu.VMEM((REACH, heads, count, 2 * dim), BF),
            pltpu.VMEM((REACH + 1, heads, count, dim), BF),
            pltpu.VMEM((REACH, heads, count), F32),
            pltpu.VMEM((REACH, heads, count), F32),
            pltpu.VMEM((2, heads, count), F32),
            pltpu.VMEM((heads, 2 * count, dim), BF),
            pltpu.VMEM((heads, 3 * count, dim + count), BF),
            pltpu.VMEM((heads, 3 * dim, dim), BF),
            pltpu.VMEM((heads, rows, 2 * dim), BF),
            pltpu.VMEM((heads, rows, count), F32),
            pltpu.VMEM((heads, rows, 2 * dim), F32),
            pltpu.VMEM((heads, rows, count), F32),
            pltpu.VMEM((rows, count), F32),
            pltpu.VMEM((rows, count), F32),
            pltpu.VMEM((8, REACH * count), F32),
            dma((heads,)),
            dma((heads,)),
            dma((REACH, CHUNKS)),
            dma((REACH, CHUNKS)),
            dma((REACH,)),
            dma((REACH,)),
            dma((REACH,)),
            dma((REACH,)),
        ],
        compiler_params=pltpu.CompilerParams(
            vmem_limit_bytes=60 << 20, collective_id=0, has_side_effects=True
        ),
    )(doc_lengths, forget_logit.T, beta, keys, values, house, queries)


def solution(mesh):
    placed = (
        P(("grp", "seq"), None, None),
        P(("grp", "seq"), None, None),
        P(("grp", "seq"), None, None),
        P(("grp", "seq"), None, None),
        P(("grp", "seq"), None),
        P(("grp", "seq"), None),
        P("grp"),
    )
    return jax.shard_map(
        shards, mesh=mesh, in_specs=placed, out_specs=P(("grp", "seq"), None, None), check_vma=False
    )
```

```python
import functools
import jax
import jax.numpy as jnp
from jax import lax
from jax.experimental import pallas as pl
from jax.experimental.pallas import tpu as pltpu
from jax.sharding import PartitionSpec as P

REACH = 4
NEG = -1e30
LOG2E = 1.4426950408889634
BF = jnp.bfloat16
F32 = jnp.float32


def halves(x):
    hi = x.astype(BF)
    return hi, (x - hi.astype(F32)).astype(BF)


def dot(a, b):
    return jnp.dot(a, b, preferred_element_type=F32)


def dot_nt(a, b):
    return lax.dot_general(a, b, (((1,), (1,)), ((), ())), preferred_element_type=F32)


def left3(x):
    hi, lo = halves(x)
    return jnp.concatenate([hi, lo, hi], axis=1)


def right3(x):
    hi, lo = halves(x)
    return jnp.concatenate([hi, hi, lo], axis=0)


def left2(x):
    hi, lo = halves(x)
    return jnp.concatenate([hi, lo], axis=1)


def inverses(systems, betas):
    length = systems[0].shape[0]
    row = lax.broadcasted_iota(jnp.int32, (length, length), 0)
    col = lax.broadcasted_iota(jnp.int32, (length, length), 1)
    heads = range(len(systems))
    invs = [jnp.where(row == col, betas[h], 0.0) for h in heads]
    first = (row + 1 == col) & (row % 2 == 0)
    rows = [jnp.sum(inv, axis=0, keepdims=True) for inv in invs]
    invs = [
        invs[h] - jnp.where(first, betas[h] * systems[h] * rows[h], 0.0) for h in heads
    ]
    width = 2
    while width < length:
        corner = (
            (row // (2 * width) == col // (2 * width))
            & (row // width % 2 == 0)
            & (col // width % 2 == 1)
        )
        links = [right3(jnp.where(corner, systems[h], 0.0)) for h in heads]
        parts = [dot(left3(invs[h]), links[h]) for h in heads]
        invs = [invs[h] - dot(left3(parts[h]), right3(invs[h])) for h in heads]
        width *= 2
    return invs


CHUNKS = 4
TILE = 256


def fused_kernel(
    docs_ref, gate_ref, beta_ref, k_ref, v_ref, u_ref, q_hbm, out_hbm,
    q_buf, o_buf, k_send, k_got, vals, b_send, b_got, tots, uks, ws, moves, qls, intras, accs, peaks,
    own_mask, row_mask, col_mask,
    q_sem, o_sem, ks_sem, kr_sem, vs_sem, vr_sem, bs_sem, br_sem,
):
    count, heads, dim = k_ref.shape
    group = q_buf.shape[2]
    rows = count * group
    span = heads // CHUNKS
    me, last = lax.axis_index("seq"), lax.axis_size("seq") - 1
    right, left = jnp.minimum(me + 1, last), jnp.maximum(me - 1, 0)
    has_right, has_left = me < last, me > 0

    def remote(src, dst, send, recv):
        return pltpu.make_async_remote_copy(
            src_ref=src, dst_ref=dst, send_sem=send, recv_sem=recv,
            device_id={"seq": right}, device_id_type=pl.DeviceIdType.MESH,
        )

    def k_copy(hop, c):
        part = pl.ds(c * span, span)
        return remote(
            k_send.at[hop - 1, part], k_got.at[hop - 1, part], ks_sem.at[hop - 1, c], kr_sem.at[hop - 1, c]
        )

    def v_copy(hop):
        return remote(vals.at[hop - 1], vals.at[hop], vs_sem.at[hop - 1], vr_sem.at[hop - 1])

    def b_copy(hop):
        return remote(b_send.at[hop - 1], b_got.at[hop - 1], bs_sem.at[hop - 1], br_sem.at[hop - 1])

    def start(copy):
        @pl.when(has_right)
        def _():
            copy.start()

    def got(copy):
        @pl.when(has_left)
        def _():
            copy.wait_recv()

    def q_copy(h):
        return pltpu.make_async_copy(q_hbm.at[:, pl.ds(h * group, group), :], q_buf.at[h], q_sem.at[h])

    def o_copy(h):
        return pltpu.make_async_copy(o_buf.at[h], out_hbm.at[:, pl.ds(h * group, group), :], o_sem.at[h])

    barrier = pltpu.get_barrier_semaphore()

    @pl.when(has_left)
    def _():
        pl.semaphore_signal(barrier, inc=1, device_id={"seq": left}, device_id_type=pl.DeviceIdType.MESH)

    @pl.when(has_right)
    def _():
        pl.semaphore_signal(barrier, inc=1, device_id={"seq": right}, device_id_type=pl.DeviceIdType.MESH)

    for h in range(heads):
        q_copy(h).start()

    @pl.when(jnp.logical_not(has_left))
    def _():
        k_got[...] = jnp.zeros_like(k_got)
        b_got[...] = jnp.zeros_like(b_got)
        vals[pl.ds(1, REACH)] = jnp.zeros((REACH,) + vals.shape[1:], BF)

    vals[0] = pltpu.einshape("mhd->hmd", v_ref[...].astype(F32)).astype(BF)
    row = lax.broadcasted_iota(jnp.int32, (count, count), 0)
    col = lax.broadcasted_iota(jnp.int32, (count, count), 1)
    logit = gate_ref[...].astype(F32)
    gate = (jnp.minimum(logit, 0.0) - jnp.log1p(jnp.exp(-jnp.abs(logit)))) * LOG2E
    g1, g2 = halves(gate)
    g3 = (gate - g1.astype(F32) - g2.astype(F32)).astype(BF)
    pieces = jnp.concatenate([g1, g2, g3], axis=1)

    def summed(mask):
        return dot(pieces, jnp.concatenate([mask.astype(F32).astype(BF)] * 3, axis=0))

    b_send[0] = summed(row > col)
    tots[0] = summed(row <= col)
    tots[1] = summed(row >= 0)

    @pl.when(has_left & has_right)
    def _():
        pl.semaphore_wait(barrier, 2)

    @pl.when(jnp.logical_not(has_left & has_right))
    def _():
        pl.semaphore_wait(barrier, 1)

    start(v_copy(1))
    start(b_copy(1))

    kf = pltpu.einshape("mhd->hmd", k_ref[...].astype(F32))
    uf = pltpu.einshape("mhd->hmd", u_ref[...].astype(F32))
    beta = beta_ref[...].astype(F32)
    us = [uf[h].astype(BF) for h in range(heads)]
    ks = [kf[h].astype(BF) for h in range(heads)]
    betas = [
        jnp.sum(jnp.where(row == col, beta[h : h + 1], 0.0), axis=1, keepdims=True)
        / (jnp.sum(uf[h] * uf[h], axis=1, keepdims=True) + 1e-06)
        for h in range(heads)
    ]
    invs = inverses([dot_nt(us[h], us[h]) for h in range(heads)], betas)
    fus = []
    for c in range(CHUNKS):
        for h in range(c * span, (c + 1) * span):
            fu = dot(left2(invs[h]), jnp.concatenate([us[h], us[h]], axis=0))
            fus.append(fu)
            proj = jnp.where(col > row, dot_nt(ks[h], us[h]), 0.0)
            hi, lo = halves(kf[h] - dot(left3(proj), right3(fu)))
            k_send[0, h] = jnp.concatenate([hi, lo], axis=1)
        start(k_copy(1, c))
    got(v_copy(1))
    start(v_copy(2))
    for h in range(heads):
        ut = uf[h].T.astype(BF)
        fhi, flo = halves(fus[h])
        move = jnp.where(row == col, 1.0, 0.0) - dot(
            jnp.concatenate([ut, ut], axis=1), jnp.concatenate([fhi, flo], axis=0)
        )
        moves[h] = right3(move)
        ft = invs[h].T
        projt = jnp.where(row > col, dot_nt(us[h], ks[h]), 0.0)
        w1 = dot(left2(ft), jnp.concatenate([us[h], us[h]], axis=0))
        w2 = dot(left3(ft), right3(projt))
        ws[h] = right3(jnp.concatenate([w1, w2], axis=1))
        uks[h] = jnp.concatenate([us[h], ks[h]], axis=0)

    token = lax.broadcasted_iota(jnp.int32, (rows, count), 0) // group
    key = lax.broadcasted_iota(jnp.int32, (rows, count), 1)
    scale = LOG2E / dim**0.5

    def query_side(h, carry):
        q_copy(h).wait()
        for at in range(0, rows, TILE):
            part = pl.ds(at, TILE)
            toks = pl.ds(at // group, TILE // group)
            qf = q_buf[h, toks].astype(F32).reshape(TILE, dim)
            both = dot_nt(qf.astype(BF), uks[h])
            proj = jnp.where(key[:TILE] <= token[at : at + TILE], both[:, :count], 0.0)
            fix = dot(left3(proj), ws[h])
            qls[h, part] = left2((qf - fix[:, :dim]) * scale)
            intras[h, part] = (both[:, count:] - fix[:, dim:]) * scale
        return carry

    def pass_on(hop, c):
        got(k_copy(hop, c))
        if hop == REACH:
            return
        for h in range(c * span, (c + 1) * span):
            x = k_got[hop - 1, h]
            hi, lo = halves(dot(jnp.concatenate([x, x[:, :dim]], axis=1), moves[h]))
            k_send[hop, h] = jnp.concatenate([hi, lo], axis=1)
        start(k_copy(hop + 1, c))

    def pass_bias(hop):
        got(b_copy(hop))
        if hop < REACH:
            b_send[hop] = b_got[hop - 1] + tots[1]
            start(b_copy(hop + 1))

    def masks():
        base = me * count

        def one(n, carry):
            begin, s_prev, e_prev, bad = carry
            end = begin + docs_ref[n]
            holds = begin < base
            s_prev = jnp.where(holds, begin, s_prev)
            e_prev = jnp.where(holds, end, e_prev)
            local = begin - base
            bad = jnp.where((token >= local) & (key < local), NEG, bad)
            return end, s_prev, e_prev, bad

        zero = jnp.int32(0)
        _, s_prev, e_prev, bad = lax.fori_loop(
            0, docs_ref.shape[0], one, (zero, zero, zero, jnp.where(key <= token, 0.0, NEG))
        )
        own_mask[...] = bad
        row_mask[...] = jnp.where(base + token < e_prev, 0.0, NEG)
        spot = lax.broadcasted_iota(jnp.int32, (8, REACH * count), 1)
        place = base - count * (1 + spot // count) + spot % count
        col_mask[...] = jnp.where(place >= s_prev, 0.0, NEG)

    def hop_keys(h, hop):
        pair = jnp.concatenate([k_got[hop - 1, h], k_got[hop, h]], axis=0)
        pair = jnp.concatenate([pair[:, :dim], pair], axis=1)
        shifts = []
        for n in range(2):
            at = (hop - 1 + n) * count
            shifts.append(b_got[hop - 1 + n, pl.ds(h, 1), :] + col_mask[0:1, at : at + count])
        return pair, shifts

    def hop_scores(h, part, pair, shifts):
        ql = qls[h, part]
        ql = jnp.concatenate([ql, ql[:, :dim]], axis=1)
        both = dot_nt(ql, pair)
        cut = row_mask[part]
        return [both[:, n * count : (n + 1) * count] + shifts[n] + cut for n in range(2)]

    def weigh(parts, peak, stack):
        his, los = [], []
        for part in parts:
            hi, lo = halves(jnp.exp2(part - peak))
            his.append(hi)
            los.append(lo)
        return dot(jnp.concatenate(his + los, axis=1), stack)

    def stacked(h, first, end):
        stack = jnp.concatenate([vals[n, h] for n in range(first, end)], axis=0)
        stack = jnp.concatenate([stack, jnp.ones_like(stack)], axis=1)
        return jnp.concatenate([stack, stack], axis=0)

    def near(h, carry):
        pair, shifts = hop_keys(h, 1)
        stack = stacked(h, 0, 3)
        own = tots[0, pl.ds(h, 1), :]
        for at in range(0, rows, TILE):
            part = pl.ds(at, TILE)
            parts = [intras[h, part] + own_mask[part] - own] + hop_scores(h, part, pair, shifts)
            peak = jnp.max(functools.reduce(jnp.maximum, parts), axis=1, keepdims=True)
            accs[h, part] = weigh(parts, peak, stack)
            peaks[h, part] = jnp.broadcast_to(peak, (TILE, count))
        return carry

    def far(h, carry):
        pair, shifts = hop_keys(h, 3)
        stack = stacked(h, 3, 5)
        for at in range(0, rows, TILE):
            part = pl.ds(at, TILE)
            parts = hop_scores(h, part, pair, shifts)
            old = peaks[h, part]
            peak = jnp.max(functools.reduce(jnp.maximum, parts + [old]), axis=1, keepdims=True)
            acc = weigh(parts, peak, stack)
            fade = jnp.exp2(old - peak)
            top = acc[:, :dim] + fade * accs[h, part, :dim]
            low = acc[:, dim:] + fade * accs[h, part, dim:]
            o_buf[h, pl.ds(at // group, TILE // group)] = (top / low).reshape(TILE // group, group, dim).astype(BF)
        o_copy(h).start()
        return carry

    def one(body, h):
        lax.fori_loop(h, h + 1, body, 0)

    lax.fori_loop(0, 2, query_side, 0)
    for c in range(CHUNKS):
        pass_on(1, c)
        if c == 0:
            pass_bias(1)
        one(query_side, 2 + c)
    got(v_copy(2))
    start(v_copy(3))
    pass_on(2, 0)
    pass_bias(2)
    one(query_side, 6)
    pass_on(2, 1)
    one(query_side, 7)
    pass_on(2, 2)
    masks()
    pass_on(2, 3)
    got(v_copy(3))
    start(v_copy(4))
    for c in range(CHUNKS):
        one(near, c)
        pass_on(3, c)
        if c == 0:
            pass_bias(3)
    lax.fori_loop(CHUNKS, heads, near, 0)
    pass_bias(4)
    got(v_copy(4))
    for c in range(CHUNKS):
        pass_on(4, c)
        lax.fori_loop(c * span, (c + 1) * span, far, 0)

    @pl.when(has_right)
    def _():
        for hop in range(1, REACH + 1):
            v_copy(hop).wait_send()
            b_copy(hop).wait_send()
            for c in range(CHUNKS):
                k_copy(hop, c).wait_send()

    for h in range(heads):
        o_copy(h).wait()


def shards(queries, keys, values, house, beta, forget_logit, doc_lengths):
    count, heads, dim = keys.shape
    group = queries.shape[1] // heads
    rows = count * group
    vmem = pl.BlockSpec(memory_space=pltpu.VMEM)
    hbm = pl.BlockSpec(memory_space=pl.ANY)
    dma = pltpu.SemaphoreType.DMA
    return pl.pallas_call(
        fused_kernel,
        in_specs=[pl.BlockSpec(memory_space=pltpu.SMEM)] + [vmem] * 5 + [hbm],
        out_specs=hbm,
        out_shape=jax.ShapeDtypeStruct(queries.shape, BF),
        scratch_shapes=[
            pltpu.VMEM((heads, count, group, dim), BF),
            pltpu.VMEM((heads, count, group, dim), BF),
            pltpu.VMEM((REACH, heads, count, 2 * dim), BF),
            pltpu.VMEM((REACH, heads, count, 2 * dim), BF),
            pltpu.VMEM((REACH + 1, heads, count, dim), BF),
            pltpu.VMEM((REACH, heads, count), F32),
            pltpu.VMEM((REACH, heads, count), F32),
            pltpu.VMEM((2, heads, count), F32),
            pltpu.VMEM((heads, 2 * count, dim), BF),
            pltpu.VMEM((heads, 3 * count, dim + count), BF),
            pltpu.VMEM((heads, 3 * dim, dim), BF),
            pltpu.VMEM((heads, rows, 2 * dim), BF),
            pltpu.VMEM((heads, rows, count), F32),
            pltpu.VMEM((heads, rows, 2 * dim), F32),
            pltpu.VMEM((heads, rows, count), F32),
            pltpu.VMEM((rows, count), F32),
            pltpu.VMEM((rows, count), F32),
            pltpu.VMEM((8, REACH * count), F32),
            dma((heads,)),
            dma((heads,)),
            dma((REACH, CHUNKS)),
            dma((REACH, CHUNKS)),
            dma((REACH,)),
            dma((REACH,)),
            dma((REACH,)),
            dma((REACH,)),
        ],
        compiler_params=pltpu.CompilerParams(
            vmem_limit_bytes=60 << 20, collective_id=0, has_side_effects=True
        ),
    )(doc_lengths, forget_logit.T, beta.T, keys, values, house, queries)


def solution(mesh):
    placed = (
        P(("grp", "seq"), None, None),
        P(("grp", "seq"), None, None),
        P(("grp", "seq"), None, None),
        P(("grp", "seq"), None, None),
        P(("grp", "seq"), None),
        P(("grp", "seq"), None),
        P("grp"),
    )
    return jax.shard_map(
        shards, mesh=mesh, in_specs=placed, out_specs=P(("grp", "seq"), None, None), check_vma=False
    )
```

```python
import functools
import jax
import jax.numpy as jnp
from jax import lax
from jax.experimental import pallas as pl
from jax.experimental.pallas import tpu as pltpu
from jax.sharding import PartitionSpec as P

REACH = 4
NEG = -1e30
LOG2E = 1.4426950408889634
BF = jnp.bfloat16
F32 = jnp.float32


def halves(x):
    hi = x.astype(BF)
    return hi, (x - hi.astype(F32)).astype(BF)


def dot(a, b):
    return jnp.dot(a, b, preferred_element_type=F32)


def dot_nt(a, b):
    return lax.dot_general(a, b, (((1,), (1,)), ((), ())), preferred_element_type=F32)


def left3(x):
    hi, lo = halves(x)
    return jnp.concatenate([hi, lo, hi], axis=1)


def right3(x):
    hi, lo = halves(x)
    return jnp.concatenate([hi, hi, lo], axis=0)


def left2(x):
    hi, lo = halves(x)
    return jnp.concatenate([hi, lo], axis=1)


def inverses(systems, betas):
    length = systems[0].shape[0]
    row = lax.broadcasted_iota(jnp.int32, (length, length), 0)
    col = lax.broadcasted_iota(jnp.int32, (length, length), 1)
    heads = range(len(systems))
    invs = [jnp.where(row == col, betas[h], 0.0) for h in heads]
    first = (row + 1 == col) & (row % 2 == 0)
    rows = [jnp.sum(inv, axis=0, keepdims=True) for inv in invs]
    invs = [
        invs[h] - jnp.where(first, betas[h] * systems[h] * rows[h], 0.0) for h in heads
    ]
    width = 2
    while width < length:
        corner = (
            (row // (2 * width) == col // (2 * width))
            & (row // width % 2 == 0)
            & (col // width % 2 == 1)
        )
        links = [right3(jnp.where(corner, systems[h], 0.0)) for h in heads]
        parts = [dot(left3(invs[h]), links[h]) for h in heads]
        invs = [invs[h] - dot(left3(parts[h]), right3(invs[h])) for h in heads]
        width *= 2
    return invs


CHUNKS = 4
TILE = 256


def fused_kernel(
    docs_ref, gate_ref, beta_ref, k_ref, v_ref, u_ref, q_hbm, out_hbm,
    q_buf, o_buf, k_send, k_got, vals, b_send, b_got, tots, uks, ws, moves, qls, intras, accs, peaks,
    own_mask, row_mask, col_mask,
    q_sem, o_sem, ks_sem, kr_sem, vs_sem, vr_sem, bs_sem, br_sem,
):
    count, heads, dim = k_ref.shape
    group = q_buf.shape[2]
    rows = count * group
    span = heads // CHUNKS
    me, last = lax.axis_index("seq"), lax.axis_size("seq") - 1
    right, left = jnp.minimum(me + 1, last), jnp.maximum(me - 1, 0)
    has_right, has_left = me < last, me > 0

    def remote(src, dst, send, recv):
        return pltpu.make_async_remote_copy(
            src_ref=src, dst_ref=dst, send_sem=send, recv_sem=recv,
            device_id={"seq": right}, device_id_type=pl.DeviceIdType.MESH,
        )

    def k_copy(hop, c):
        part = pl.ds(c * span, span)
        return remote(
            k_send.at[hop - 1, part], k_got.at[hop - 1, part], ks_sem.at[hop - 1, c], kr_sem.at[hop - 1, c]
        )

    def v_copy(hop):
        return remote(vals.at[hop - 1], vals.at[hop], vs_sem.at[hop - 1], vr_sem.at[hop - 1])

    def b_copy(hop):
        return remote(b_send.at[hop - 1], b_got.at[hop - 1], bs_sem.at[hop - 1], br_sem.at[hop - 1])

    def start(copy):
        @pl.when(has_right)
        def _():
            copy.start()

    def got(copy):
        @pl.when(has_left)
        def _():
            copy.wait_recv()

    def q_copy(h):
        return pltpu.make_async_copy(q_hbm.at[:, pl.ds(h * group, group), :], q_buf.at[h], q_sem.at[h])

    def o_copy(h):
        return pltpu.make_async_copy(o_buf.at[h], out_hbm.at[:, pl.ds(h * group, group), :], o_sem.at[h])

    barrier = pltpu.get_barrier_semaphore()

    @pl.when(has_left)
    def _():
        pl.semaphore_signal(barrier, inc=1, device_id={"seq": left}, device_id_type=pl.DeviceIdType.MESH)

    @pl.when(has_right)
    def _():
        pl.semaphore_signal(barrier, inc=1, device_id={"seq": right}, device_id_type=pl.DeviceIdType.MESH)

    for h in range(heads):
        q_copy(h).start()

    @pl.when(jnp.logical_not(has_left))
    def _():
        k_got[...] = jnp.zeros_like(k_got)
        b_got[...] = jnp.zeros_like(b_got)
        vals[pl.ds(1, REACH)] = jnp.zeros((REACH,) + vals.shape[1:], BF)

    vals[0] = pltpu.einshape("mhd->hmd", v_ref[...].astype(F32)).astype(BF)
    row = lax.broadcasted_iota(jnp.int32, (count, count), 0)
    col = lax.broadcasted_iota(jnp.int32, (count, count), 1)
    logit = gate_ref[...].astype(F32)
    gate = (jnp.minimum(logit, 0.0) - jnp.log1p(jnp.exp(-jnp.abs(logit)))) * LOG2E
    g1, g2 = halves(gate)
    g3 = (gate - g1.astype(F32) - g2.astype(F32)).astype(BF)
    pieces = jnp.concatenate([g1, g2, g3], axis=1)

    def summed(mask):
        return dot(pieces, jnp.concatenate([mask.astype(F32).astype(BF)] * 3, axis=0))

    b_send[0] = summed(row > col)
    tots[0] = summed(row <= col)
    tots[1] = summed(row >= 0)

    @pl.when(has_left & has_right)
    def _():
        pl.semaphore_wait(barrier, 2)

    @pl.when(jnp.logical_not(has_left & has_right))
    def _():
        pl.semaphore_wait(barrier, 1)

    start(v_copy(1))
    start(b_copy(1))

    kf = pltpu.einshape("mhd->hmd", k_ref[...].astype(F32))
    uf = pltpu.einshape("mhd->hmd", u_ref[...].astype(F32))
    beta = beta_ref[...].astype(F32)
    us = [uf[h].astype(BF) for h in range(heads)]
    ks = [kf[h].astype(BF) for h in range(heads)]
    betas = [
        jnp.sum(jnp.where(row == col, beta[h : h + 1], 0.0), axis=1, keepdims=True)
        / (jnp.sum(uf[h] * uf[h], axis=1, keepdims=True) + 1e-06)
        for h in range(heads)
    ]
    invs = inverses([dot_nt(us[h], us[h]) for h in range(heads)], betas)
    fus = []
    for c in range(CHUNKS):
        for h in range(c * span, (c + 1) * span):
            fu = dot(left2(invs[h]), jnp.concatenate([us[h], us[h]], axis=0))
            fus.append(fu)
            proj = jnp.where(col > row, dot_nt(ks[h], us[h]), 0.0)
            hi, lo = halves(kf[h] - dot(left3(proj), right3(fu)))
            k_send[0, h] = jnp.concatenate([hi, lo], axis=1)
        start(k_copy(1, c))
    got(v_copy(1))
    start(v_copy(2))
    for h in range(heads):
        ut = uf[h].T.astype(BF)
        fhi, flo = halves(fus[h])
        move = jnp.where(row == col, 1.0, 0.0) - dot(
            jnp.concatenate([ut, ut], axis=1), jnp.concatenate([fhi, flo], axis=0)
        )
        moves[h] = right3(move)
        ft = invs[h].T
        projt = jnp.where(row > col, dot_nt(us[h], ks[h]), 0.0)
        w1 = dot(left2(ft), jnp.concatenate([us[h], us[h]], axis=0))
        w2 = dot(left3(ft), right3(projt))
        ws[h] = right3(jnp.concatenate([w1, w2], axis=1))
        uks[h] = jnp.concatenate([us[h], ks[h]], axis=0)

    token = lax.broadcasted_iota(jnp.int32, (rows, count), 0) // group
    key = lax.broadcasted_iota(jnp.int32, (rows, count), 1)
    scale = LOG2E / dim**0.5

    def query_side(h, carry):
        q_copy(h).wait()
        for at in range(0, rows, TILE):
            part = pl.ds(at, TILE)
            toks = pl.ds(at // group, TILE // group)
            qf = q_buf[h, toks].astype(F32).reshape(TILE, dim)
            both = dot_nt(qf.astype(BF), uks[h])
            proj = jnp.where(key[:TILE] <= token[at : at + TILE], both[:, :count], 0.0)
            fix = dot(left3(proj), ws[h])
            qls[h, part] = left2((qf - fix[:, :dim]) * scale)
            intras[h, part] = (both[:, count:] - fix[:, dim:]) * scale
        return carry

    def pass_on(hop, c):
        got(k_copy(hop, c))
        if hop == REACH:
            return
        for h in range(c * span, (c + 1) * span):
            x = k_got[hop - 1, h]
            hi, lo = halves(dot(jnp.concatenate([x, x[:, :dim]], axis=1), moves[h]))
            k_send[hop, h] = jnp.concatenate([hi, lo], axis=1)
        start(k_copy(hop + 1, c))

    def pass_bias(hop):
        got(b_copy(hop))
        if hop < REACH:
            b_send[hop] = b_got[hop - 1] + tots[1]
            start(b_copy(hop + 1))

    def masks():
        base = me * count

        def one(n, carry):
            begin, s_prev, e_prev, bad = carry
            end = begin + docs_ref[n]
            holds = begin < base
            s_prev = jnp.where(holds, begin, s_prev)
            e_prev = jnp.where(holds, end, e_prev)
            local = begin - base
            bad = jnp.where((token >= local) & (key < local), NEG, bad)
            return end, s_prev, e_prev, bad

        zero = jnp.int32(0)
        _, s_prev, e_prev, bad = lax.fori_loop(
            0, docs_ref.shape[0], one, (zero, zero, zero, jnp.where(key <= token, 0.0, NEG))
        )
        own_mask[...] = bad
        row_mask[...] = jnp.where(base + token < e_prev, 0.0, NEG)
        spot = lax.broadcasted_iota(jnp.int32, (8, REACH * count), 1)
        place = base - count * (1 + spot // count) + spot % count
        col_mask[...] = jnp.where(place >= s_prev, 0.0, NEG)

    def hop_keys(h, hop):
        pair = jnp.concatenate([k_got[hop - 1, h], k_got[hop, h]], axis=0)
        pair = jnp.concatenate([pair[:, :dim], pair], axis=1)
        shifts = []
        for n in range(2):
            at = (hop - 1 + n) * count
            shifts.append(b_got[hop - 1 + n, pl.ds(h, 1), :] + col_mask[0:1, at : at + count])
        return pair, shifts

    def hop_scores(h, part, pair, shifts):
        ql = qls[h, part]
        ql = jnp.concatenate([ql, ql[:, :dim]], axis=1)
        both = dot_nt(ql, pair)
        cut = row_mask[part]
        return [both[:, n * count : (n + 1) * count] + shifts[n] + cut for n in range(2)]

    def weigh(parts, peak, stack):
        his, los = [], []
        for part in parts:
            hi, lo = halves(jnp.exp2(part - peak))
            his.append(hi)
            los.append(lo)
        return dot(jnp.concatenate(his + los, axis=1), stack)

    def stacked(h, first, end):
        stack = jnp.concatenate([vals[n, h] for n in range(first, end)], axis=0)
        stack = jnp.concatenate([stack, jnp.ones_like(stack)], axis=1)
        return jnp.concatenate([stack, stack], axis=0)

    def near(h, carry):
        pair, shifts = hop_keys(h, 1)
        stack = stacked(h, 0, 3)
        own = tots[0, pl.ds(h, 1), :]
        for at in range(0, rows, TILE):
            part = pl.ds(at, TILE)
            parts = [intras[h, part] + own_mask[part] - own] + hop_scores(h, part, pair, shifts)
            peak = jnp.max(functools.reduce(jnp.maximum, parts), axis=1, keepdims=True)
            accs[h, part] = weigh(parts, peak, stack)
            peaks[h, part] = jnp.broadcast_to(peak, (TILE, count))
        return carry

    def far(h, carry):
        pair, shifts = hop_keys(h, 3)
        stack = stacked(h, 3, 5)
        for at in range(0, rows, TILE):
            part = pl.ds(at, TILE)
            parts = hop_scores(h, part, pair, shifts)
            old = peaks[h, part]
            peak = jnp.max(functools.reduce(jnp.maximum, parts + [old]), axis=1, keepdims=True)
            acc = weigh(parts, peak, stack)
            fade = jnp.exp2(old - peak)
            top = acc[:, :dim] + fade * accs[h, part, :dim]
            low = acc[:, dim:] + fade * accs[h, part, dim:]
            o_buf[h, pl.ds(at // group, TILE // group)] = (top / low).reshape(TILE // group, group, dim).astype(BF)
        o_copy(h).start()
        return carry

    def one(body, h):
        lax.fori_loop(h, h + 1, body, 0)

    one(query_side, 0)
    for c in range(CHUNKS):
        pass_on(1, c)
        if c == 0:
            pass_bias(1)
        one(query_side, 1 + c)
    pass_on(2, 0)
    pass_bias(2)
    got(v_copy(2))
    start(v_copy(3))
    for c in range(1, CHUNKS):
        one(query_side, CHUNKS + c)
        pass_on(2, c)
    masks()
    got(v_copy(3))
    start(v_copy(4))
    for c in range(CHUNKS):
        one(near, c)
        pass_on(3, c)
        if c == 0:
            pass_bias(3)
    lax.fori_loop(CHUNKS, heads, near, 0)
    pass_bias(4)
    got(v_copy(4))
    for c in range(CHUNKS):
        pass_on(4, c)
        lax.fori_loop(c * span, (c + 1) * span, far, 0)

    @pl.when(has_right)
    def _():
        for hop in range(1, REACH + 1):
            v_copy(hop).wait_send()
            b_copy(hop).wait_send()
            for c in range(CHUNKS):
                k_copy(hop, c).wait_send()

    for h in range(heads):
        o_copy(h).wait()


def shards(queries, keys, values, house, beta, forget_logit, doc_lengths):
    count, heads, dim = keys.shape
    group = queries.shape[1] // heads
    rows = count * group
    vmem = pl.BlockSpec(memory_space=pltpu.VMEM)
    hbm = pl.BlockSpec(memory_space=pl.ANY)
    dma = pltpu.SemaphoreType.DMA
    return pl.pallas_call(
        fused_kernel,
        in_specs=[pl.BlockSpec(memory_space=pltpu.SMEM)] + [vmem] * 5 + [hbm],
        out_specs=hbm,
        out_shape=jax.ShapeDtypeStruct(queries.shape, BF),
        scratch_shapes=[
            pltpu.VMEM((heads, count, group, dim), BF),
            pltpu.VMEM((heads, count, group, dim), BF),
            pltpu.VMEM((REACH, heads, count, 2 * dim), BF),
            pltpu.VMEM((REACH, heads, count, 2 * dim), BF),
            pltpu.VMEM((REACH + 1, heads, count, dim), BF),
            pltpu.VMEM((REACH, heads, count), F32),
            pltpu.VMEM((REACH, heads, count), F32),
            pltpu.VMEM((2, heads, count), F32),
            pltpu.VMEM((heads, 2 * count, dim), BF),
            pltpu.VMEM((heads, 3 * count, dim + count), BF),
            pltpu.VMEM((heads, 3 * dim, dim), BF),
            pltpu.VMEM((heads, rows, 2 * dim), BF),
            pltpu.VMEM((heads, rows, count), F32),
            pltpu.VMEM((heads, rows, 2 * dim), F32),
            pltpu.VMEM((heads, rows, count), F32),
            pltpu.VMEM((rows, count), F32),
            pltpu.VMEM((rows, count), F32),
            pltpu.VMEM((8, REACH * count), F32),
            dma((heads,)),
            dma((heads,)),
            dma((REACH, CHUNKS)),
            dma((REACH, CHUNKS)),
            dma((REACH,)),
            dma((REACH,)),
            dma((REACH,)),
            dma((REACH,)),
        ],
        compiler_params=pltpu.CompilerParams(
            vmem_limit_bytes=60 << 20, collective_id=0, has_side_effects=True
        ),
    )(doc_lengths, forget_logit.T, beta.T, keys, values, house, queries)


def solution(mesh):
    placed = (
        P(("grp", "seq"), None, None),
        P(("grp", "seq"), None, None),
        P(("grp", "seq"), None, None),
        P(("grp", "seq"), None, None),
        P(("grp", "seq"), None),
        P(("grp", "seq"), None),
        P("grp"),
    )
    return jax.shard_map(
        shards, mesh=mesh, in_specs=placed, out_specs=P(("grp", "seq"), None, None), check_vma=False
    )
```
